32 devices in a mesh: slab: 16 (over z, y, x), pencil: 2 (over core).
Axes of the slice: x: 2, y: 2, z: 4, core: 2. Of those that a mesh axis runs over, the one named last changes fastest.
Arguments:
- owner_map: int32 [16], replicated, may hold values from 0 to 15
- window_start: int32 [1], replicated, may hold values from 0 to 8
- child_maps: float32 [8, 20, 20], replicated, may hold values from -1 to 1
- innovation: float32 [20, 20], replicated, may hold values from -1.25 to 1.25
- coarse_bank: float32 [16, 20, 74898], P('slab'), may hold values from -6 to 6
- noise_middle: float32 [20, 64, 64, 128], P(None, 'slab', 'pencil'), may hold values from -6 to 6
- noise_finest: float32 [20, 128, 128, 256], P(None, 'slab', 'pencil'), may hold values from -6 to 6
Outputs:
- field_values: float32 [256, 256, 512], P('slab', 'pencil')
- zface_mean: float32 [128, 256, 512], P('slab', 'pencil')
- yface_mean: float32 [256, 128, 512], P('slab', 'pencil')
The draws below stay inside these ranges and needn't reach their ends.
All inputs are finite; a program needn't handle non-finite values.
Results may differ from the reference program's by a relative error of at most 0.0001.
Values sent between devices are 32-bit elements; how exact they have to be, the bound alone decides.
A program may use at most 448 MiB of HBM per device.

```python
import math
import jax
import jax.numpy as jnp
import numpy as np
from jax import lax

K = 20
LEVELS = 8
ROOTS = 2
ROOTS_Z = 1
ROOTS_Y = 1
DEPTH = 16
COARSE = 74898
FZ = 128
FY = 128
FX = 256
N_SLAB = 16


def touch_ends(result, rng, least, top_value):
    spot = [jax.random.randint(jax.random.fold_in(rng, axis), (), 0, length) for axis, length in enumerate(result.shape)]
    widest = result.shape.index(max(result.shape))
    beside = spot[:widest] + [(spot[widest] + 1) % result.shape[widest]] + spot[widest + 1:]
    return result.at[tuple(spot)].set(least).at[tuple(beside)].set(top_value)


def steps_of(rng, dims, split, least, largest):
    level = 1.0
    for dim, shards_of in split:
        heights = jax.random.uniform(jax.random.fold_in(jax.random.fold_in(rng, 6), dim), (shards_of,), jnp.float32, least / len(split), largest / len(split))
        level = level * jnp.repeat(jnp.exp(heights), dims[dim] // shards_of).reshape((-1,) + (1,) * (len(dims) - 1 - dim))
    return level


def bell_draw(rng, shape, width, bound, cuts=(), kind=jnp.bfloat16):
    entries = width * jax.random.normal(rng, shape, jnp.float32)
    if cuts:
        entries = entries * steps_of(rng, shape, cuts, -0.22, 0.18)
    return jnp.clip(entries, -bound, bound).astype(kind)


def setup_inputs(seed: int = 0) -> dict:
    seeds = jax.random.split(jax.random.key(seed), 8)
    owner_map = touch_ends(jax.random.randint(seeds[0], (DEPTH,), 0, N_SLAB), jax.random.fold_in(seeds[0], 1), 0, N_SLAB - 1).astype(jnp.int32)
    window_start = jax.random.randint(seeds[1], (1,), 0, DEPTH - LEVELS + 1).astype(jnp.int32)
    child_maps = bell_draw(seeds[2], (8, K, K), (2 * K) ** -0.5, 1.0, (), jnp.float32)
    innovation = bell_draw(seeds[3], (K, K), K ** -0.5, 1.25, (), jnp.float32)
    coarse_bank = bell_draw(seeds[4], (N_SLAB, K, COARSE), 1.0, 6.0, ((0, 16),), jnp.float32)
    noise_middle = bell_draw(seeds[5], (K, FZ // 2, FY // 2, FX // 2), 1.0, 6.0, ((1, 16), (2, 2)), jnp.float32)
    noise_finest = bell_draw(seeds[6], (K, FZ, FY, FX), 1.0, 6.0, ((1, 16), (2, 2)), jnp.float32)
    return {"owner_map": owner_map, "window_start": window_start, "child_maps": child_maps, "innovation": innovation, "coarse_bank": coarse_bank, "noise_middle": noise_middle, "noise_finest": noise_finest}


def legendre(order, point):
    values = [1.0, point, 1.5 * point * point - 0.5, 2.5 * point * point * point - 1.5 * point]
    return values[order]

def basis_table(points):
    table_rows = []
    for point in points:
        w_coord, v_coord, u_coord = point
        entry = []
        for deg_x in range(4):
            for deg_y in range(4):
                for deg_z in range(4):
                    if deg_x + deg_y + deg_z <= 3:
                        factor = math.sqrt((2 * deg_x + 1) * (2 * deg_y + 1) * (2 * deg_z + 1))
                        entry.append(factor * legendre(deg_x, u_coord) * legendre(deg_y, v_coord) * legendre(deg_z, w_coord))
        table_rows.append(entry)
    return jnp.asarray(np.array(table_rows), jnp.float32)

def level_block(flat, level):
    scale = 2 ** level
    first = ROOTS_Z * ROOTS_Y * ROOTS
    offset = first * (8 ** level - 1) // 7
    length = first * 8 ** level
    return flat[:, offset:offset + length].reshape(flat.shape[0], ROOTS_Z * scale, ROOTS_Y * scale, ROOTS * scale)

def descend(parent, child_maps):
    kids = jnp.einsum('okn,nzyx->okzyx', child_maps, parent, precision=lax.Precision.HIGHEST)
    count, planes, rows_y, cols_x = parent.shape
    kids = kids.reshape(2, 2, 2, count, planes, rows_y, cols_x).transpose(3, 4, 0, 5, 1, 6, 2)
    return kids.reshape(count, 2 * planes, 2 * rows_y, 2 * cols_x)

def innovate(innovation, noise):
    return jnp.einsum('kn,nzyx->kzyx', innovation, noise, precision=lax.Precision.HIGHEST)

def expand(table, coeffs):
    return jnp.einsum('pk,kzyx->pzyx', table, coeffs, precision=lax.Precision.HIGHEST)

def reference(owner_map, window_start, child_maps, innovation, coarse_bank, noise_middle, noise_finest):
    coeffs = None
    for level in range(LEVELS - 2):
        owner = owner_map[window_start[0] + level].astype(jnp.int32)
        chosen = lax.dynamic_index_in_dim(coarse_bank, owner, 0, keepdims=False)
        fresh = innovate(innovation, level_block(chosen, level))
        coeffs = fresh if level == 0 else descend(coeffs, child_maps) + fresh
    coeffs = descend(coeffs, child_maps) + innovate(innovation, noise_middle)
    fine = descend(coeffs, child_maps) + innovate(innovation, noise_finest)
    count, planes, rows_y, cols_x = fine.shape
    halves = [-0.5, 0.5]
    inner = basis_table([(pz, py, px) for pz in halves for py in halves for px in halves])
    top = basis_table([(1.0, py, px) for py in halves for px in halves])
    bottom = basis_table([(-1.0, py, px) for py in halves for px in halves])
    north = basis_table([(pz, 1.0, px) for pz in halves for px in halves])
    south = basis_table([(pz, -1.0, px) for pz in halves for px in halves])
    values = expand(inner, fine).reshape(2, 2, 2, planes, rows_y, cols_x).transpose(3, 0, 4, 1, 5, 2)
    field_values = values.reshape(2 * planes, 2 * rows_y, 2 * cols_x)
    zsum = expand(top, fine) + jnp.roll(expand(bottom, fine), -1, axis=1)
    zface = (0.5 * zsum).reshape(2, 2, planes, rows_y, cols_x).transpose(2, 3, 0, 4, 1)
    zface_mean = zface.reshape(planes, 2 * rows_y, 2 * cols_x)
    ysum = expand(north, fine) + jnp.roll(expand(south, fine), -1, axis=2)
    yface = (0.5 * ysum).reshape(2, 2, planes, rows_y, cols_x).transpose(2, 0, 3, 4, 1)
    yface_mean = yface.reshape(2 * planes, rows_y, 2 * cols_x)
    return (field_values, zface_mean, yface_mean)
```

```python
import functools
import math

import jax
import jax.numpy as jnp
import numpy as np
from jax import lax
from jax.experimental import pallas as pl
from jax.experimental.pallas import tpu as pltpu
from jax.sharding import PartitionSpec as P

LEVELS = 8
ROOTS = 2
BANKS = LEVELS - 2
LANES = 128
F32 = jnp.float32
BF16 = jnp.bfloat16
HI = lax.Precision.HIGHEST


def legendre(order, point):
    values = [1.0, point, 1.5 * point * point - 0.5, 2.5 * point * point * point - 1.5 * point]
    return values[order]


def basis_row(point):
    w_coord, v_coord, u_coord = point
    entry = []
    for deg_x in range(4):
        for deg_y in range(4):
            for deg_z in range(4):
                if deg_x + deg_y + deg_z <= 3:
                    factor = math.sqrt((2 * deg_x + 1) * (2 * deg_y + 1) * (2 * deg_z + 1))
                    entry.append(
                        factor
                        * legendre(deg_x, u_coord)
                        * legendre(deg_y, v_coord)
                        * legendre(deg_z, w_coord)
                    )
    return np.array(entry)


def shifted(block, axis, distance):
    devices = range(lax.axis_size(axis))
    route = [((i - distance) % len(devices), i) for i in devices]
    return lax.ppermute(block, axis, route)


def offset_of(level):
    return ROOTS * (8**level - 1) // 7


def round_up(size, unit):
    return -(-size // unit) * unit


class Region:
    def __init__(self, level, n_slab, n_pencil):
        side = 2**level
        self.level = level
        self.nx = ROOTS * side
        self.plane = side * self.nx
        self.whole = self.plane % LANES != 0
        rows = max(1, side // n_pencil)
        self.split = (not self.whole) and (rows * self.nx) % LANES == 0
        self.ny = rows if self.split else side
        self.nz = side if self.whole else max(1, side // n_slab)
        self.count = self.nz * self.ny * self.nx
        self.padded = round_up(self.count, LANES)
        self.n_slab = n_slab
        self.side = side

    def first_plane(self, slab):
        return 0 * slab if self.whole else (slab * self.side) // self.n_slab

    def first_row(self, pencil):
        return pencil * self.ny if self.split else 0 * pencil


def regions_of(n_slab, n_pencil):
    regions = [Region(level, n_slab, n_pencil) for level in range(BANKS)]
    head = [r for r in regions if r.whole]
    tail = [r for r in regions if not r.whole]
    head_width = round_up(offset_of(len(head)), LANES)
    width = head_width
    for r in tail:
        r.start = width
        width += r.count
    return regions, head, tail, head_width, width


def prep_kernel(n_slab, n_pencil, info, bank, out, end):
    regions, head, tail, head_width, width = regions_of(n_slab, n_pencil)
    step = pl.program_id(0)
    pencil = info[0]
    total = bank.shape[2]
    last = total // LANES * LANES
    count = bank.shape[1]

    @pl.when(step == 0)
    def _():
        end[...] = jnp.zeros_like(end)
        if total > last:
            end[:, : total - last] = bank[0, :, last:total]

    lane = lax.broadcasted_iota(jnp.int32, (count, head_width), 1)
    own = jnp.zeros((count, head_width), jnp.int32)
    for r in head:
        own = jnp.where((lane >= offset_of(r.level)), info[1 + r.level], own)
    out[0, :, :head_width] = jnp.where(own > 0, bank[0, :, :head_width], 0.0)
    lanes = lax.broadcasted_iota(jnp.int32, (count, LANES), 1)
    for r in tail:
        shift = offset_of(r.level) % LANES
        owned = info[1 + r.level] > 0
        pieces = r.nz if r.split else 1
        size = r.count // pieces
        for z in range(pieces):
            first = (
                offset_of(r.level) - shift
                + (r.first_plane(step) + z) * r.plane
                + r.first_row(pencil) * r.nx
            )
            chunks = []
            for c in range(size // LANES + 1):
                at = first + c * LANES
                safe = pl.multiple_of(jnp.minimum(at, last - LANES), LANES)
                chunk = bank[0, :, pl.ds(safe, LANES)]
                if c == size // LANES:
                    chunk = jnp.where(at >= last, end[...], chunk)
                chunks.append(pltpu.roll(chunk, (LANES - shift) % LANES, 1))
            for c in range(size // LANES):
                piece = jnp.where(lanes < LANES - shift, chunks[c], chunks[c + 1])
                base = r.start + z * size + c * LANES
                out[0, :, base : base + LANES] = jnp.where(owned, piece, 0.0)


def split2(value):
    high = value.astype(BF16)
    low = (value - high.astype(F32)).astype(BF16)
    return high, low


def dot(left, right):
    return jnp.dot(left, right, preferred_element_type=F32)


def chain_kernel(n_slab, n_pencil, info, received, w_high, w_low, out, noise):
    regions, head, tail, head_width, width = regions_of(n_slab, n_pencil)
    slab, pencil = info[0], info[1]
    count = received.shape[0]
    padded_count = round_up(count, 8)
    noise[...] = jnp.zeros_like(noise)
    noise[:count, :] = received[...]
    parent = None
    for r in regions:
        if r.whole:
            block = noise[:, :head_width]
            start = offset_of(r.level)
            if start:
                block = pltpu.roll(block, head_width - start, 1)
            block = block[:, : r.padded]
        else:
            block = noise[:, r.start : r.start + r.padded]
        if parent is None:
            spread = jnp.zeros((8 * padded_count, r.padded), F32)
        else:
            q = regions[r.level - 1]

            def cells(shape, dim):
                cell = lax.broadcasted_iota(jnp.int32, shape, dim)
                log = lambda n: int(math.log2(n))
                x = cell & (r.nx - 1)
                y = ((cell >> log(r.nx)) & (r.ny - 1)) + r.first_row(pencil)
                z = (cell >> log(r.nx * r.ny)) + r.first_plane(slab)
                return x, y, z

            x, y, z = cells((q.padded, r.padded), 1)
            source = (
                ((z >> 1) - q.first_plane(slab)) * (q.ny * q.nx)
                + ((y >> 1) - q.first_row(pencil)) * q.nx
                + (x >> 1)
            )
            pick = jnp.where(
                lax.broadcasted_iota(jnp.int32, (q.padded, r.padded), 0) == source, 1.0, 0.0
            ).astype(BF16)
            p1, p2 = split2(parent)
            p3 = (parent - p1.astype(F32) - p2.astype(F32)).astype(BF16)
            up = dot(p1, pick) + dot(p2, pick) + dot(p3, pick)
            up = up[:padded_count]
            x, y, z = cells((padded_count, r.padded), 1)
            octant = 4 * (z & 1) + 2 * (y & 1) + (x & 1)
            spread = jnp.concatenate(
                [jnp.where(octant == o, up, 0.0) for o in range(8)], axis=0
            )
        stack = jnp.concatenate([spread, block], axis=0)
        high, low = split2(stack)
        parent = dot(w_high[...], high) + dot(w_high[...], low) + dot(w_low[...], high)
    out[...] = parent


def upsampled(parent, cols):
    lanes = parent.shape[1]
    source = lax.broadcasted_iota(jnp.int32, (lanes, 2 * cols), 0)
    target = lax.broadcasted_iota(jnp.int32, (lanes, 2 * cols), 1)
    wanted = jnp.where(target < cols, 2 * source, 2 * source + 1 + cols)
    pick = jnp.where(wanted == target, 1.0, 0.0).astype(BF16)
    high, low = split2(parent)
    up_high = dot(high, pick).astype(BF16)
    up_low = dot(low, pick).astype(BF16)
    return (up_high[:, :cols], up_high[:, cols:]), (up_low[:, :cols], up_low[:, cols:])


def product(weights, noise, highs, lows):
    noise_high, noise_low = split2(noise)
    high = [noise_high, *highs]
    low = [noise_low, *lows]
    return dot(weights, jnp.concatenate(high + low + high, axis=0))


def middle_kernel(per, info, upper, noise, weights, out):
    count, _, rows, lanes = upper.shape
    cols = noise.shape[3]
    highs, lows = upsampled(upper[:, 0].reshape(count * rows, lanes), cols)
    for i in range(per):
        octz = i if per == 2 else info[0]
        result = product(
            weights[octz], noise[:, i].reshape(count * 2 * rows, cols), highs, lows
        )
        out[:, i] = result.reshape(count, 2 * rows, cols)


def interleave(even, odd):
    rows, cols = even.shape
    lane = lax.broadcasted_iota(jnp.int32, (rows, LANES), 1)
    half = lane >> 1
    first = (lane & 1) == 0
    parts = []
    for j in range(2 * cols // LANES):
        at = (j // 2) * LANES
        index = half + (j % 2) * (LANES // 2)
        a = jnp.take_along_axis(even[:, at : at + LANES], index, axis=1)
        b = jnp.take_along_axis(odd[:, at : at + LANES], index, axis=1)
        parts.append(jnp.where(first, a, b))
    return jnp.concatenate(parts, axis=1)


def fine_kernel(
    middle, noise, weights, field, zface, yface, lower, south, carry_z, carry_y
):
    count, _, rows, lanes = middle.shape
    cols = noise.shape[3]
    tile = 2 * rows
    depth_step, row_step = pl.program_id(0), pl.program_id(1)

    @pl.when(depth_step == 0)
    def _():
        carry_z[row_step] = jnp.zeros(carry_z.shape[1:], F32)

    @pl.when(row_step == 0)
    def _():
        carry_y[...] = jnp.zeros_like(carry_y)

    highs, lows = upsampled(middle[:, 0].reshape(count * rows, lanes), cols)
    above = carry_z[row_step]
    row = lax.broadcasted_iota(jnp.int32, (tile, 2 * cols), 0)
    for octz in (1, 0):
        result = product(
            weights[octz], noise[:, octz].reshape(count * tile, cols), highs, lows
        )
        at = 0

        def pair(size):
            nonlocal at
            even = result[at : at + size]
            odd = result[at + size : at + 2 * size]
            at += 2 * size
            return interleave(even, odd)

        for half in range(2):
            field[2 * octz + half] = pair(2 * tile)
        zface[octz] = pair(2 * tile) + above
        above = pair(2 * tile)
        for half in range(2):
            value = pair(tile)
            edge = carry_y[octz, half : half + 1, :]
            yface[2 * octz + half] = value + jnp.where(row == tile - 1, edge, 0.0)
        edge = pair(8)
        carry_y[octz] = edge
        south[0, octz] = edge
    carry_z[row_step] = above
    lower[...] = above


def fine_rows(tile):
    table, index = [], {}

    def entry(point, scale):
        key = (point, scale)
        if key not in index:
            index[key] = len(table)
            table.append(scale * basis_row(point))
        return index[key]

    halves = [-0.5, 0.5]
    rows = []
    for pz in halves:
        for px in halves:
            for y in range(tile):
                for py in halves:
                    rows.append([(entry((pz, py, px), 1.0), y)])
    for w in (1.0, -1.0):
        for px in halves:
            for y in range(tile):
                for py in halves:
                    rows.append([(entry((w, py, px), 0.5), y)])
    for pz in halves:
        for px in halves:
            for y in range(tile):
                terms = [(entry((pz, 1.0, px), 0.5), y)]
                if y + 1 < tile:
                    terms.append((entry((pz, -1.0, px), 0.5), y + 1))
                rows.append(terms)
    for px in halves:
        for pz in halves:
            rows.append([(entry((pz, -1.0, px), 0.5), 0)])
        rows.extend([[]] * 6)
    return np.array(table), rows


def packed_weights(table, rows, tile, child_maps, innovation):
    count = innovation.shape[0]
    entries = table.shape[0]
    columns = 2 * count * tile
    chan = np.zeros((3 * count, columns), np.float32)
    fine_y = np.zeros((columns,), np.int64)
    is_noise = np.zeros((columns,), bool)
    c = 0
    for block, size in ((0, tile), (1, tile // 2), (2, tile // 2)):
        for k in range(count):
            for y in range(size):
                chan[block * count + k, c] = 1
                fine_y[c] = y
                is_noise[c] = block == 0
                c += 1
    picks, masks = [], []
    for term in range(max(len(r) for r in rows)):
        pick = np.zeros((len(rows), 2 * entries), np.float32)
        mask = np.zeros((len(rows), columns), bool)
        for i, terms in enumerate(rows):
            if term < len(terms):
                q, y = terms[term]
                pick[i, (y % 2) * entries + q] = 1
                mask[i] = np.where(is_noise, fine_y == y, fine_y == y // 2)
        picks.append(pick)
        masks.append(mask)
    table = jnp.asarray(table, F32)
    own = jnp.dot(table, innovation, precision=HI)
    maps = jnp.einsum("qk,okn->oqn", table, child_maps, precision=HI)
    out = []
    for octz in range(2):
        small = jnp.concatenate(
            [
                jnp.concatenate(
                    [own, maps[4 * octz + 2 * octy], maps[4 * octz + 2 * octy + 1]], axis=1
                )
                for octy in range(2)
            ],
            axis=0,
        )
        wide = jnp.dot(small, jnp.asarray(chan), precision=HI)
        total = 0.0
        for pick, mask in zip(picks, masks):
            part = jnp.dot(jnp.asarray(pick), wide, precision=HI)
            total = total + jnp.where(jnp.asarray(mask), part, 0.0)
        out.append(total)
    full = jnp.stack(out)
    high = lax.reduce_precision(full, 8, 7)
    low = full - high
    return jnp.concatenate([high, high, low], axis=2).astype(BF16)


def shards(n_slab, n_pencil, owner_map, window_start, child_maps, innovation, bank,
           noise_middle, noise_finest):
    slab = lax.axis_index("slab").astype(jnp.int32)
    pencil = lax.axis_index("pencil").astype(jnp.int32)
    regions, head, tail, head_width, width = regions_of(n_slab, n_pencil)
    count = innovation.shape[0]
    owners = lax.dynamic_slice(owner_map, (window_start[0],), (BANKS,))
    info = jnp.concatenate([pencil[None], (owners == slab).astype(jnp.int32)])
    smem = pl.BlockSpec(memory_space=pltpu.SMEM)
    windows = pl.pallas_call(
        functools.partial(prep_kernel, n_slab, n_pencil),
        grid=(n_slab,),
        in_specs=[smem, pl.BlockSpec(bank.shape, lambda s: (0, 0, 0))],
        out_specs=pl.BlockSpec((1, count, width), lambda s: (s, 0, 0)),
        out_shape=jax.ShapeDtypeStruct((n_slab, count, width), F32),
        scratch_shapes=[pltpu.VMEM((count, LANES), F32)],
        name="windows",
    )(info, bank)
    received = lax.psum_scatter(windows, "slab", scatter_dimension=0, tiled=True)[0]

    padded = round_up(count, 8)
    wide = round_up(padded, 16)
    maps = jnp.pad(child_maps, ((0, 0), (0, wide - count), (0, padded - count)))
    flat = jnp.concatenate(
        [maps[o] for o in range(8)]
        + [jnp.pad(innovation, ((0, wide - count), (0, wide - count)))],
        axis=1,
    )
    flat_high = lax.reduce_precision(flat, 8, 7)
    place = jnp.stack([slab, pencil])
    vmem = pl.BlockSpec(memory_space=pltpu.VMEM)
    top = regions[-1]
    upper = pl.pallas_call(
        functools.partial(chain_kernel, n_slab, n_pencil),
        in_specs=[smem, vmem, vmem, vmem],
        out_specs=vmem,
        out_shape=jax.ShapeDtypeStruct((wide, top.padded), F32),
        scratch_shapes=[pltpu.VMEM((wide, width), F32)],
        name="coarse",
    )(place, received, flat_high.astype(BF16), (flat - flat_high).astype(BF16))
    upper = upper[:count].reshape(count, top.nz, top.ny, top.nx)

    tile = 16
    half = tile // 2
    eye_rows = [[(k, y)] for k in range(count) for y in range(tile)]
    middle_weights = packed_weights(np.eye(count), eye_rows, tile, child_maps, innovation)
    _, planes, rows, cols = noise_middle.shape
    per = planes // top.nz
    octz = (slab * planes) % 2
    middle = pl.pallas_call(
        functools.partial(middle_kernel, per),
        grid=(top.nz, rows // tile),
        in_specs=[
            smem,
            pl.BlockSpec((count, 1, half, top.nx), lambda z, y: (0, z, y, 0)),
            pl.BlockSpec((count, per, tile, cols), lambda z, y: (0, z, y, 0)),
            vmem,
        ],
        out_specs=pl.BlockSpec((count, per, tile, cols), lambda z, y: (0, z, y, 0)),
        out_shape=jax.ShapeDtypeStruct(noise_middle.shape, F32),
        name="middle",
    )(octz[None], upper, noise_middle, middle_weights)

    table, row_list = fine_rows(tile)
    fine_weights = packed_weights(table, row_list, tile, child_maps, innovation)
    _, fine_planes, fine_y, fine_x = noise_finest.shape
    nz, ny = planes, fine_y // tile
    out_x = 2 * fine_x

    def block(*where):
        def index(z, y):
            at = {"z": nz - 1 - z, "y": ny - 1 - y}
            return tuple(at.get(w, 0) for w in where)

        return index

    field, zface, yface, lower, south = pl.pallas_call(
        fine_kernel,
        grid=(nz, ny),
        in_specs=[
            pl.BlockSpec((count, 1, half, cols), block(0, "z", "y", 0)),
            pl.BlockSpec((count, 2, tile, fine_x), block(0, "z", "y", 0)),
            vmem,
        ],
        out_specs=[
            pl.BlockSpec((4, 2 * tile, out_x), block("z", "y", 0)),
            pl.BlockSpec((2, 2 * tile, out_x), block("z", "y", 0)),
            pl.BlockSpec((4, tile, out_x), block("z", "y", 0)),
            pl.BlockSpec((2 * tile, out_x), block("y", 0)),
            pl.BlockSpec((1, 2, 8, out_x), block("z", 0, 0, 0)),
        ],
        out_shape=[
            jax.ShapeDtypeStruct((2 * fine_planes, 2 * fine_y, out_x), F32),
            jax.ShapeDtypeStruct((fine_planes, 2 * fine_y, out_x), F32),
            jax.ShapeDtypeStruct((2 * fine_planes, fine_y, out_x), F32),
            jax.ShapeDtypeStruct((2 * fine_y, out_x), F32),
            jax.ShapeDtypeStruct((nz, 2, 8, out_x), F32),
        ],
        scratch_shapes=[
            pltpu.VMEM((ny, 2 * tile, out_x), F32),
            pltpu.VMEM((2, 8, out_x), F32),
        ],
        name="fine",
    )(middle, noise_finest, fine_weights)
    above = shifted(lower, "slab", -1)
    beside = shifted(south[:, :, :2].reshape(2 * fine_planes, out_x), "pencil", -1)
    zface = zface.at[-1].add(above)
    yface = yface.at[:, -1].add(beside)
    return field, zface, yface


def solution(mesh):
    placed = (
        P(),
        P(),
        P(),
        P(),
        P("slab", None, None),
        P(None, "slab", "pencil", None),
        P(None, "slab", "pencil", None),
    )
    return jax.shard_map(
        functools.partial(shards, mesh.shape["slab"], mesh.shape["pencil"]),
        mesh=mesh,
        in_specs=placed,
        out_specs=(P("slab", "pencil", None), P("slab", "pencil", None), P("slab", "pencil", None)),
        check_vma=False,
    )
```

```python
import functools
import math

import jax
import jax.numpy as jnp
import numpy as np
from jax import lax
from jax.experimental import pallas as pl
from jax.experimental.pallas import tpu as pltpu
from jax.sharding import PartitionSpec as P

LEVELS = 8
ROOTS = 2
BANKS = LEVELS - 2
LANES = 128
F32 = jnp.float32
BF16 = jnp.bfloat16
HI = lax.Precision.HIGHEST


def legendre(order, point):
    values = [1.0, point, 1.5 * point * point - 0.5, 2.5 * point * point * point - 1.5 * point]
    return values[order]


def basis_row(point):
    w_coord, v_coord, u_coord = point
    entry = []
    for deg_x in range(4):
        for deg_y in range(4):
            for deg_z in range(4):
                if deg_x + deg_y + deg_z <= 3:
                    factor = math.sqrt((2 * deg_x + 1) * (2 * deg_y + 1) * (2 * deg_z + 1))
                    entry.append(
                        factor
                        * legendre(deg_x, u_coord)
                        * legendre(deg_y, v_coord)
                        * legendre(deg_z, w_coord)
                    )
    return np.array(entry)


def shifted(block, axis, distance):
    devices = range(lax.axis_size(axis))
    route = [((i - distance) % len(devices), i) for i in devices]
    return lax.ppermute(block, axis, route)


def offset_of(level):
    return ROOTS * (8**level - 1) // 7


def round_up(size, unit):
    return -(-size // unit) * unit


class Region:
    def __init__(self, level, n_slab, n_pencil):
        side = 2**level
        self.level = level
        self.nx = ROOTS * side
        self.plane = side * self.nx
        self.whole = self.plane % LANES != 0
        rows = max(1, side // n_pencil)
        self.split = (not self.whole) and (rows * self.nx) % LANES == 0
        self.ny = rows if self.split else side
        self.nz = side if self.whole else max(1, side // n_slab)
        self.count = self.nz * self.ny * self.nx
        self.padded = round_up(self.count, LANES)
        self.n_slab = n_slab
        self.side = side

    def first_plane(self, slab):
        return 0 * slab if self.whole else (slab * self.side) // self.n_slab

    def first_row(self, pencil):
        return pencil * self.ny if self.split else 0 * pencil


def regions_of(n_slab, n_pencil):
    regions = [Region(level, n_slab, n_pencil) for level in range(BANKS)]
    head = [r for r in regions if r.whole]
    tail = [r for r in regions if not r.whole]
    head_width = round_up(offset_of(len(head)), LANES)
    width = head_width
    for r in tail:
        r.start = width
        width += r.count
    return regions, head, tail, head_width, width


def prep_kernel(n_slab, n_pencil, info, bank, out, end):
    regions, head, tail, head_width, width = regions_of(n_slab, n_pencil)
    step = pl.program_id(0)
    pencil = info[0]
    total = bank.shape[2]
    last = total // LANES * LANES
    count = bank.shape[1]

    @pl.when(step == 0)
    def _():
        end[...] = jnp.zeros_like(end)
        if total > last:
            end[:, : total - last] = bank[0, :, last:total]

    lane = lax.broadcasted_iota(jnp.int32, (count, head_width), 1)
    own = jnp.zeros((count, head_width), jnp.int32)
    for r in head:
        own = jnp.where((lane >= offset_of(r.level)), info[1 + r.level], own)
    out[0, :, :head_width] = jnp.where(own > 0, bank[0, :, :head_width], 0.0)
    lanes = lax.broadcasted_iota(jnp.int32, (count, LANES), 1)
    for r in tail:
        shift = offset_of(r.level) % LANES
        owned = info[1 + r.level] > 0
        pieces = r.nz if r.split else 1
        size = r.count // pieces
        for z in range(pieces):
            first = (
                offset_of(r.level) - shift
                + (r.first_plane(step) + z) * r.plane
                + r.first_row(pencil) * r.nx
            )
            chunks = []
            for c in range(size // LANES + 1):
                at = first + c * LANES
                safe = pl.multiple_of(jnp.minimum(at, last - LANES), LANES)
                chunk = bank[0, :, pl.ds(safe, LANES)]
                if c == size // LANES:
                    chunk = jnp.where(at >= last, end[...], chunk)
                chunks.append(pltpu.roll(chunk, (LANES - shift) % LANES, 1))
            for c in range(size // LANES):
                piece = jnp.where(lanes < LANES - shift, chunks[c], chunks[c + 1])
                base = r.start + z * size + c * LANES
                out[0, :, base : base + LANES] = jnp.where(owned, piece, 0.0)


def split2(value):
    high = value.astype(BF16)
    low = (value - high.astype(F32)).astype(BF16)
    return high, low


def dot(left, right):
    return jnp.dot(left, right, preferred_element_type=F32)


def chain_kernel(n_slab, n_pencil, info, received, w_high, w_low, out, noise):
    regions, head, tail, head_width, width = regions_of(n_slab, n_pencil)
    slab, pencil = info[0], info[1]
    count = received.shape[0]
    padded_count = round_up(count, 8)
    noise[...] = jnp.zeros_like(noise)
    noise[:count, :] = received[...]
    parent = None
    for r in regions:
        if r.whole:
            block = noise[:, :head_width]
            start = offset_of(r.level)
            if start:
                block = pltpu.roll(block, head_width - start, 1)
            block = block[:, : r.padded]
        else:
            block = noise[:, r.start : r.start + r.padded]
        if parent is None:
            spread = jnp.zeros((8 * padded_count, r.padded), F32)
        else:
            q = regions[r.level - 1]

            def cells(shape, dim):
                cell = lax.broadcasted_iota(jnp.int32, shape, dim)
                log = lambda n: int(math.log2(n))
                x = cell & (r.nx - 1)
                y = ((cell >> log(r.nx)) & (r.ny - 1)) + r.first_row(pencil)
                z = (cell >> log(r.nx * r.ny)) + r.first_plane(slab)
                return x, y, z

            x, y, z = cells((q.padded, r.padded), 1)
            source = (
                ((z >> 1) - q.first_plane(slab)) * (q.ny * q.nx)
                + ((y >> 1) - q.first_row(pencil)) * q.nx
                + (x >> 1)
            )
            pick = jnp.where(
                lax.broadcasted_iota(jnp.int32, (q.padded, r.padded), 0) == source, 1.0, 0.0
            ).astype(BF16)
            p1, p2 = split2(parent)
            p3 = (parent - p1.astype(F32) - p2.astype(F32)).astype(BF16)
            up = dot(p1, pick) + dot(p2, pick) + dot(p3, pick)
            up = up[:padded_count]
            x, y, z = cells((padded_count, r.padded), 1)
            octant = 4 * (z & 1) + 2 * (y & 1) + (x & 1)
            spread = jnp.concatenate(
                [jnp.where(octant == o, up, 0.0) for o in range(8)], axis=0
            )
        stack = jnp.concatenate([spread, block], axis=0)
        high, low = split2(stack)
        parent = dot(w_high[...], high) + dot(w_high[...], low) + dot(w_low[...], high)
    out[...] = parent


def upsampled(parent, cols):
    lanes = parent.shape[1]
    source = lax.broadcasted_iota(jnp.int32, (lanes, 2 * cols), 0)
    target = lax.broadcasted_iota(jnp.int32, (lanes, 2 * cols), 1)
    wanted = jnp.where(target < cols, 2 * source, 2 * source + 1 + cols)
    pick = jnp.where(wanted == target, 1.0, 0.0).astype(BF16)
    high, low = split2(parent)
    up_high = dot(high, pick).astype(BF16)
    up_low = dot(low, pick).astype(BF16)
    return (up_high[:, :cols], up_high[:, cols:]), (up_low[:, :cols], up_low[:, cols:])


def product(weights, noise, highs, lows):
    noise_high, noise_low = split2(noise)
    high = [noise_high, *highs]
    low = [noise_low, *lows]
    return dot(weights, jnp.concatenate(high + low + high, axis=0))


def middle_kernel(per, info, upper, noise, weights, out):
    count, _, rows, lanes = upper.shape
    cols = noise.shape[3]
    highs, lows = upsampled(upper[:, 0].reshape(count * rows, lanes), cols)
    for i in range(per):
        octz = i if per == 2 else info[0]
        result = product(
            weights[octz], noise[:, i].reshape(count * 2 * rows, cols), highs, lows
        )
        out[:, i] = result.reshape(count, 2 * rows, cols)


def interleave(even, odd):
    rows, cols = even.shape
    lane = lax.broadcasted_iota(jnp.int32, (rows, LANES), 1)
    half = lane >> 1
    first = (lane & 1) == 0
    parts = []
    for j in range(2 * cols // LANES):
        at = (j // 2) * LANES
        index = half + (j % 2) * (LANES // 2)
        a = jnp.take_along_axis(even[:, at : at + LANES], index, axis=1)
        b = jnp.take_along_axis(odd[:, at : at + LANES], index, axis=1)
        parts.append(jnp.where(first, a, b))
    return jnp.concatenate(parts, axis=1)


def fine_kernel(
    middle, noise, weights, field, zface, yface, lower, south, carry_z, carry_y
):
    count, _, rows, lanes = middle.shape
    cols = noise.shape[3]
    tile = 2 * rows
    depth_step, row_step = pl.program_id(0), pl.program_id(1)

    @pl.when(depth_step == 0)
    def _():
        carry_z[row_step] = jnp.zeros(carry_z.shape[1:], F32)

    @pl.when(row_step == 0)
    def _():
        carry_y[...] = jnp.zeros_like(carry_y)

    highs, lows = upsampled(middle[:, 0].reshape(count * rows, lanes), cols)
    above = carry_z[row_step]
    row = lax.broadcasted_iota(jnp.int32, (tile, 2 * cols), 0)
    for octz in (1, 0):
        result = product(
            weights[octz], noise[:, octz].reshape(count * tile, cols), highs, lows
        )
        at = 0

        def pair(size):
            nonlocal at
            even = result[at : at + size]
            odd = result[at + size : at + 2 * size]
            at += 2 * size
            return interleave(even, odd)

        for half in range(2):
            field[2 * octz + half] = pair(2 * tile)
        zface[octz] = pair(2 * tile) + above
        above = pair(2 * tile)
        for half in range(2):
            value = pair(tile)
            edge = carry_y[octz, half : half + 1, :]
            yface[2 * octz + half] = value + jnp.where(row == tile - 1, edge, 0.0)
        edge = pair(8)
        carry_y[octz] = edge
        south[0, octz] = edge
    carry_z[row_step] = above
    lower[...] = above


def fine_rows(tile):
    table, index = [], {}

    def entry(point, scale):
        key = (point, scale)
        if key not in index:
            index[key] = len(table)
            table.append(scale * basis_row(point))
        return index[key]

    halves = [-0.5, 0.5]
    rows = []
    for pz in halves:
        for px in halves:
            for y in range(tile):
                for py in halves:
                    rows.append([(entry((pz, py, px), 1.0), y)])
    for w in (1.0, -1.0):
        for px in halves:
            for y in range(tile):
                for py in halves:
                    rows.append([(entry((w, py, px), 0.5), y)])
    for pz in halves:
        for px in halves:
            for y in range(tile):
                terms = [(entry((pz, 1.0, px), 0.5), y)]
                if y + 1 < tile:
                    terms.append((entry((pz, -1.0, px), 0.5), y + 1))
                rows.append(terms)
    for px in halves:
        for pz in halves:
            rows.append([(entry((pz, -1.0, px), 0.5), 0)])
        rows.extend([[]] * 6)
    return np.array(table), rows


def packed_weights(table, rows, tile, child_maps, innovation):
    count = innovation.shape[0]
    entries = table.shape[0]
    columns = 2 * count * tile
    chan = np.zeros((3 * count, columns), np.float32)
    fine_y = np.zeros((columns,), np.int64)
    is_noise = np.zeros((columns,), bool)
    c = 0
    for block, size in ((0, tile), (1, tile // 2), (2, tile // 2)):
        for k in range(count):
            for y in range(size):
                chan[block * count + k, c] = 1
                fine_y[c] = y
                is_noise[c] = block == 0
                c += 1
    picks, masks = [], []
    for term in range(max(len(r) for r in rows)):
        pick = np.zeros((len(rows), 2 * entries), np.float32)
        mask = np.zeros((len(rows), columns), bool)
        for i, terms in enumerate(rows):
            if term < len(terms):
                q, y = terms[term]
                pick[i, (y % 2) * entries + q] = 1
                mask[i] = np.where(is_noise, fine_y == y, fine_y == y // 2)
        picks.append(pick)
        masks.append(mask)
    table = jnp.asarray(table, F32)
    own = jnp.dot(table, innovation, precision=HI)
    maps = jnp.einsum("qk,okn->oqn", table, child_maps, precision=HI)
    out = []
    for octz in range(2):
        small = jnp.concatenate(
            [
                jnp.concatenate(
                    [own, maps[4 * octz + 2 * octy], maps[4 * octz + 2 * octy + 1]], axis=1
                )
                for octy in range(2)
            ],
            axis=0,
        )
        wide = jnp.dot(small, jnp.asarray(chan), precision=HI)
        total = 0.0
        for pick, mask in zip(picks, masks):
            part = jnp.dot(jnp.asarray(pick), wide, precision=HI)
            total = total + jnp.where(jnp.asarray(mask), part, 0.0)
        out.append(total)
    full = jnp.stack(out)
    high = lax.reduce_precision(full, 8, 7)
    low = full - high
    return jnp.concatenate([high, high, low], axis=2).astype(BF16)


def shards(n_slab, n_pencil, owner_map, window_start, child_maps, innovation, bank,
           noise_middle, noise_finest):
    slab = lax.axis_index("slab").astype(jnp.int32)
    pencil = lax.axis_index("pencil").astype(jnp.int32)
    regions, head, tail, head_width, width = regions_of(n_slab, n_pencil)
    count = innovation.shape[0]
    owners = lax.dynamic_slice(owner_map, (window_start[0],), (BANKS,))
    info = jnp.concatenate([pencil[None], (owners == slab).astype(jnp.int32)])
    smem = pl.BlockSpec(memory_space=pltpu.SMEM)
    inner = 1
    while inner * inner < n_slab:
        inner *= 2
    outer = n_slab // inner
    windows = pl.pallas_call(
        functools.partial(prep_kernel, n_slab, n_pencil),
        grid=(n_slab,),
        in_specs=[smem, pl.BlockSpec(bank.shape, lambda s: (0, 0, 0))],
        out_specs=pl.BlockSpec(
            (1, count, width), lambda s: ((s % inner) * outer + s // inner, 0, 0)
        ),
        out_shape=jax.ShapeDtypeStruct((n_slab, count, width), F32),
        scratch_shapes=[pltpu.VMEM((count, LANES), F32)],
        name="windows",
    )(info, bank)
    near = [[o * inner + i for i in range(inner)] for o in range(outer)]
    far = [[o * inner + i for o in range(outer)] for i in range(inner)]
    parts = windows.reshape(inner, outer, count, width)
    parts = lax.all_to_all(parts, "slab", 0, 0, axis_index_groups=near, tiled=True)
    parts = jnp.sum(parts, axis=0)
    parts = lax.all_to_all(parts, "slab", 0, 0, axis_index_groups=far, tiled=True)
    received = jnp.sum(parts, axis=0)

    padded = round_up(count, 8)
    wide = round_up(padded, 16)
    maps = jnp.pad(child_maps, ((0, 0), (0, wide - count), (0, padded - count)))
    flat = jnp.concatenate(
        [maps[o] for o in range(8)]
        + [jnp.pad(innovation, ((0, wide - count), (0, wide - count)))],
        axis=1,
    )
    flat_high = lax.reduce_precision(flat, 8, 7)
    place = jnp.stack([slab, pencil])
    vmem = pl.BlockSpec(memory_space=pltpu.VMEM)
    top = regions[-1]
    upper = pl.pallas_call(
        functools.partial(chain_kernel, n_slab, n_pencil),
        in_specs=[smem, vmem, vmem, vmem],
        out_specs=vmem,
        out_shape=jax.ShapeDtypeStruct((wide, top.padded), F32),
        scratch_shapes=[pltpu.VMEM((wide, width), F32)],
        name="coarse",
    )(place, received, flat_high.astype(BF16), (flat - flat_high).astype(BF16))
    upper = upper[:count].reshape(count, top.nz, top.ny, top.nx)

    tile = 16
    half = tile // 2
    eye_rows = [[(k, y)] for k in range(count) for y in range(tile)]
    middle_weights = packed_weights(np.eye(count), eye_rows, tile, child_maps, innovation)
    _, planes, rows, cols = noise_middle.shape
    per = planes // top.nz
    octz = (slab * planes) % 2
    middle = pl.pallas_call(
        functools.partial(middle_kernel, per),
        grid=(top.nz, rows // tile),
        in_specs=[
            smem,
            pl.BlockSpec((count, 1, half, top.nx), lambda z, y: (0, z, y, 0)),
            pl.BlockSpec((count, per, tile, cols), lambda z, y: (0, z, y, 0)),
            vmem,
        ],
        out_specs=pl.BlockSpec((count, per, tile, cols), lambda z, y: (0, z, y, 0)),
        out_shape=jax.ShapeDtypeStruct(noise_middle.shape, F32),
        name="middle",
    )(octz[None], upper, noise_middle, middle_weights)

    table, row_list = fine_rows(tile)
    fine_weights = packed_weights(table, row_list, tile, child_maps, innovation)
    _, fine_planes, fine_y, fine_x = noise_finest.shape
    nz, ny = planes, fine_y // tile
    out_x = 2 * fine_x

    def block(*where):
        def index(z, y):
            at = {"z": nz - 1 - z, "y": ny - 1 - y}
            return tuple(at.get(w, 0) for w in where)

        return index

    field, zface, yface, lower, south = pl.pallas_call(
        fine_kernel,
        grid=(nz, ny),
        in_specs=[
            pl.BlockSpec((count, 1, half, cols), block(0, "z", "y", 0)),
            pl.BlockSpec((count, 2, tile, fine_x), block(0, "z", "y", 0)),
            vmem,
        ],
        out_specs=[
            pl.BlockSpec((4, 2 * tile, out_x), block("z", "y", 0)),
            pl.BlockSpec((2, 2 * tile, out_x), block("z", "y", 0)),
            pl.BlockSpec((4, tile, out_x), block("z", "y", 0)),
            pl.BlockSpec((2 * tile, out_x), block("y", 0)),
            pl.BlockSpec((1, 2, 8, out_x), block("z", 0, 0, 0)),
        ],
        out_shape=[
            jax.ShapeDtypeStruct((2 * fine_planes, 2 * fine_y, out_x), F32),
            jax.ShapeDtypeStruct((fine_planes, 2 * fine_y, out_x), F32),
            jax.ShapeDtypeStruct((2 * fine_planes, fine_y, out_x), F32),
            jax.ShapeDtypeStruct((2 * fine_y, out_x), F32),
            jax.ShapeDtypeStruct((nz, 2, 8, out_x), F32),
        ],
        scratch_shapes=[
            pltpu.VMEM((ny, 2 * tile, out_x), F32),
            pltpu.VMEM((2, 8, out_x), F32),
        ],
        name="fine",
    )(middle, noise_finest, fine_weights)
    above = shifted(lower, "slab", -1)
    beside = shifted(south[:, :, :2].reshape(2 * fine_planes, out_x), "pencil", -1)
    zface = zface.at[-1].add(above)
    yface = yface.at[:, -1].add(beside)
    return field, zface, yface


def solution(mesh):
    placed = (
        P(),
        P(),
        P(),
        P(),
        P("slab", None, None),
        P(None, "slab", "pencil", None),
        P(None, "slab", "pencil", None),
    )
    return jax.shard_map(
        functools.partial(shards, mesh.shape["slab"], mesh.shape["pencil"]),
        mesh=mesh,
        in_specs=placed,
        out_specs=(P("slab", "pencil", None), P("slab", "pencil", None), P("slab", "pencil", None)),
        check_vma=False,
    )
```

```python
import functools
import math

import jax
import jax.numpy as jnp
import numpy as np
from jax import lax
from jax.experimental import pallas as pl
from jax.experimental.pallas import tpu as pltpu
from jax.sharding import PartitionSpec as P

LEVELS = 8
ROOTS = 2
BANKS = LEVELS - 2
LANES = 128
F32 = jnp.float32
BF16 = jnp.bfloat16
HI = lax.Precision.HIGHEST


def legendre(order, point):
    values = [1.0, point, 1.5 * point * point - 0.5, 2.5 * point * point * point - 1.5 * point]
    return values[order]


def basis_row(point):
    w_coord, v_coord, u_coord = point
    entry = []
    for deg_x in range(4):
        for deg_y in range(4):
            for deg_z in range(4):
                if deg_x + deg_y + deg_z <= 3:
                    factor = math.sqrt((2 * deg_x + 1) * (2 * deg_y + 1) * (2 * deg_z + 1))
                    entry.append(
                        factor
                        * legendre(deg_x, u_coord)
                        * legendre(deg_y, v_coord)
                        * legendre(deg_z, w_coord)
                    )
    return np.array(entry)


def shifted(block, axis, distance):
    devices = range(lax.axis_size(axis))
    route = [((i - distance) % len(devices), i) for i in devices]
    return lax.ppermute(block, axis, route)


def offset_of(level):
    return ROOTS * (8**level - 1) // 7


def round_up(size, unit):
    return -(-size // unit) * unit


class Region:
    def __init__(self, level, n_slab, n_pencil):
        side = 2**level
        self.level = level
        self.nx = ROOTS * side
        self.plane = side * self.nx
        self.whole = self.plane % LANES != 0
        rows = max(1, side // n_pencil)
        self.split = (not self.whole) and (rows * self.nx) % LANES == 0
        self.ny = rows if self.split else side
        self.nz = side if self.whole else max(1, side // n_slab)
        self.count = self.nz * self.ny * self.nx
        self.padded = round_up(self.count, LANES)
        self.n_slab = n_slab
        self.side = side

    def first_plane(self, slab):
        return 0 * slab if self.whole else (slab * self.side) // self.n_slab

    def first_row(self, pencil):
        return pencil * self.ny if self.split else 0 * pencil


def regions_of(n_slab, n_pencil):
    regions = [Region(level, n_slab, n_pencil) for level in range(BANKS)]
    head = [r for r in regions if r.whole]
    tail = [r for r in regions if not r.whole]
    head_width = round_up(offset_of(len(head)), LANES)
    width = head_width
    for r in tail:
        r.start = width
        width += r.count
    return regions, head, tail, head_width, width


def prep_kernel(n_slab, n_pencil, cut, info, bank, out, rest, end):
    regions, head, tail, head_width, width = regions_of(n_slab, n_pencil)
    step = pl.program_id(0)
    pencil = info[0]
    total = bank.shape[2]
    last = total // LANES * LANES
    count = bank.shape[1]

    @pl.when(step == 0)
    def _():
        end[...] = jnp.zeros_like(end)
        if total > last:
            end[:, : total - last] = bank[0, :, last:total]

    lane = lax.broadcasted_iota(jnp.int32, (count, head_width), 1)
    own = jnp.zeros((count, head_width), jnp.int32)
    for r in head:
        own = jnp.where((lane >= offset_of(r.level)), info[1 + r.level], own)
    out[0, :, :head_width] = jnp.where(own > 0, bank[0, :, :head_width], 0.0)
    lanes = lax.broadcasted_iota(jnp.int32, (count, LANES), 1)
    for r in tail:
        shift = offset_of(r.level) % LANES
        owned = info[1 + r.level] > 0
        pieces = r.nz if r.split else 1
        size = r.count // pieces
        for z in range(pieces):
            first = (
                offset_of(r.level) - shift
                + (r.first_plane(step) + z) * r.plane
                + r.first_row(pencil) * r.nx
            )
            chunks = []
            for c in range(size // LANES + 1):
                at = first + c * LANES
                safe = pl.multiple_of(jnp.minimum(at, last - LANES), LANES)
                chunk = bank[0, :, pl.ds(safe, LANES)]
                if c == size // LANES:
                    chunk = jnp.where(at >= last, end[...], chunk)
                chunks.append(pltpu.roll(chunk, (LANES - shift) % LANES, 1))
            for c in range(size // LANES):
                piece = jnp.where(lanes < LANES - shift, chunks[c], chunks[c + 1])
                base = r.start + z * size + c * LANES
                target, base = (out, base) if base < cut else (rest, base - cut)
                target[0, :, base : base + LANES] = jnp.where(owned, piece, 0.0)


def split2(value):
    high = value.astype(BF16)
    low = (value - high.astype(F32)).astype(BF16)
    return high, low


def dot(left, right):
    return jnp.dot(left, right, preferred_element_type=F32)


def chain_kernel(n_slab, n_pencil, info, received, w_high, w_low, out, noise):
    regions, head, tail, head_width, width = regions_of(n_slab, n_pencil)
    slab, pencil = info[0], info[1]
    count = received.shape[0]
    padded_count = round_up(count, 8)
    noise[...] = jnp.zeros_like(noise)
    noise[:count, :] = received[...]
    parent = None
    for r in regions:
        if r.whole:
            block = noise[:, :head_width]
            start = offset_of(r.level)
            if start:
                block = pltpu.roll(block, head_width - start, 1)
            block = block[:, : r.padded]
        else:
            block = noise[:, r.start : r.start + r.padded]
        if parent is None:
            spread = jnp.zeros((8 * padded_count, r.padded), F32)
        else:
            q = regions[r.level - 1]

            def cells(shape, dim):
                cell = lax.broadcasted_iota(jnp.int32, shape, dim)
                log = lambda n: int(math.log2(n))
                x = cell & (r.nx - 1)
                y = ((cell >> log(r.nx)) & (r.ny - 1)) + r.first_row(pencil)
                z = (cell >> log(r.nx * r.ny)) + r.first_plane(slab)
                return x, y, z

            x, y, z = cells((q.padded, r.padded), 1)
            source = (
                ((z >> 1) - q.first_plane(slab)) * (q.ny * q.nx)
                + ((y >> 1) - q.first_row(pencil)) * q.nx
                + (x >> 1)
            )
            pick = jnp.where(
                lax.broadcasted_iota(jnp.int32, (q.padded, r.padded), 0) == source, 1.0, 0.0
            ).astype(BF16)
            p1, p2 = split2(parent)
            p3 = (parent - p1.astype(F32) - p2.astype(F32)).astype(BF16)
            up = dot(p1, pick) + dot(p2, pick) + dot(p3, pick)
            up = up[:padded_count]
            x, y, z = cells((padded_count, r.padded), 1)
            octant = 4 * (z & 1) + 2 * (y & 1) + (x & 1)
            spread = jnp.concatenate(
                [jnp.where(octant == o, up, 0.0) for o in range(8)], axis=0
            )
        stack = jnp.concatenate([spread, block], axis=0)
        high, low = split2(stack)
        parent = dot(w_high[...], high) + dot(w_high[...], low) + dot(w_low[...], high)
    out[...] = parent


def upsampled(parent, cols):
    lanes = parent.shape[1]
    source = lax.broadcasted_iota(jnp.int32, (lanes, 2 * cols), 0)
    target = lax.broadcasted_iota(jnp.int32, (lanes, 2 * cols), 1)
    wanted = jnp.where(target < cols, 2 * source, 2 * source + 1 + cols)
    pick = jnp.where(wanted == target, 1.0, 0.0).astype(BF16)
    high, low = split2(parent)
    up_high = dot(high, pick).astype(BF16)
    up_low = dot(low, pick).astype(BF16)
    return (up_high[:, :cols], up_high[:, cols:]), (up_low[:, :cols], up_low[:, cols:])


def product(weights, noise, highs, lows):
    noise_high, noise_low = split2(noise)
    high = [noise_high, *highs]
    low = [noise_low, *lows]
    return dot(weights, jnp.concatenate(high + low + high, axis=0))


def middle_kernel(per, info, upper, noise, weights, out):
    count, _, rows, lanes = upper.shape
    cols = noise.shape[3]
    highs, lows = upsampled(upper[:, 0].reshape(count * rows, lanes), cols)
    for i in range(per):
        octz = i if per == 2 else info[0]
        result = product(
            weights[octz], noise[:, i].reshape(count * 2 * rows, cols), highs, lows
        )
        out[:, i] = result.reshape(count, 2 * rows, cols)


def interleave(even, odd):
    rows, cols = even.shape
    lane = lax.broadcasted_iota(jnp.int32, (rows, LANES), 1)
    half = lane >> 1
    first = (lane & 1) == 0
    parts = []
    for j in range(2 * cols // LANES):
        at = (j // 2) * LANES
        index = half + (j % 2) * (LANES // 2)
        a = jnp.take_along_axis(even[:, at : at + LANES], index, axis=1)
        b = jnp.take_along_axis(odd[:, at : at + LANES], index, axis=1)
        parts.append(jnp.where(first, a, b))
    return jnp.concatenate(parts, axis=1)


def fine_kernel(
    middle, noise, weights, field, zface, yface, lower, south, carry_z, carry_y
):
    count, _, rows, lanes = middle.shape
    cols = noise.shape[3]
    tile = 2 * rows
    depth_step, row_step = pl.program_id(0), pl.program_id(1)

    @pl.when(depth_step == 0)
    def _():
        carry_z[row_step] = jnp.zeros(carry_z.shape[1:], F32)

    @pl.when(row_step == 0)
    def _():
        carry_y[...] = jnp.zeros_like(carry_y)

    highs, lows = upsampled(middle[:, 0].reshape(count * rows, lanes), cols)
    above = carry_z[row_step]
    row = lax.broadcasted_iota(jnp.int32, (tile, 2 * cols), 0)
    for octz in (1, 0):
        result = product(
            weights[octz], noise[:, octz].reshape(count * tile, cols), highs, lows
        )
        at = 0

        def pair(size):
            nonlocal at
            even = result[at : at + size]
            odd = result[at + size : at + 2 * size]
            at += 2 * size
            return interleave(even, odd)

        for half in range(2):
            field[2 * octz + half] = pair(2 * tile)
        zface[octz] = pair(2 * tile) + above
        above = pair(2 * tile)
        for half in range(2):
            value = pair(tile)
            edge = carry_y[octz, half : half + 1, :]
            yface[2 * octz + half] = value + jnp.where(row == tile - 1, edge, 0.0)
        edge = pair(8)
        carry_y[octz] = edge
        south[0, octz] = edge
    carry_z[row_step] = above
    lower[...] = above


def fine_rows(tile):
    table, index = [], {}

    def entry(point, scale):
        key = (point, scale)
        if key not in index:
            index[key] = len(table)
            table.append(scale * basis_row(point))
        return index[key]

    halves = [-0.5, 0.5]
    rows = []
    for pz in halves:
        for px in halves:
            for y in range(tile):
                for py in halves:
                    rows.append([(entry((pz, py, px), 1.0), y)])
    for w in (1.0, -1.0):
        for px in halves:
            for y in range(tile):
                for py in halves:
                    rows.append([(entry((w, py, px), 0.5), y)])
    for pz in halves:
        for px in halves:
            for y in range(tile):
                terms = [(entry((pz, 1.0, px), 0.5), y)]
                if y + 1 < tile:
                    terms.append((entry((pz, -1.0, px), 0.5), y + 1))
                rows.append(terms)
    for px in halves:
        for pz in halves:
            rows.append([(entry((pz, -1.0, px), 0.5), 0)])
        rows.extend([[]] * 6)
    return np.array(table), rows


def packed_weights(table, rows, tile, child_maps, innovation):
    count = innovation.shape[0]
    entries = table.shape[0]
    columns = 2 * count * tile
    chan = np.zeros((3 * count, columns), np.float32)
    fine_y = np.zeros((columns,), np.int64)
    is_noise = np.zeros((columns,), bool)
    c = 0
    for block, size in ((0, tile), (1, tile // 2), (2, tile // 2)):
        for k in range(count):
            for y in range(size):
                chan[block * count + k, c] = 1
                fine_y[c] = y
                is_noise[c] = block == 0
                c += 1
    picks, masks = [], []
    for term in range(max(len(r) for r in rows)):
        pick = np.zeros((len(rows), 2 * entries), np.float32)
        mask = np.zeros((len(rows), columns), bool)
        for i, terms in enumerate(rows):
            if term < len(terms):
                q, y = terms[term]
                pick[i, (y % 2) * entries + q] = 1
                mask[i] = np.where(is_noise, fine_y == y, fine_y == y // 2)
        picks.append(pick)
        masks.append(mask)
    table = jnp.asarray(table, F32)
    own = jnp.dot(table, innovation, precision=HI)
    maps = jnp.einsum("qk,okn->oqn", table, child_maps, precision=HI)
    out = []
    for octz in range(2):
        small = jnp.concatenate(
            [
                jnp.concatenate(
                    [own, maps[4 * octz + 2 * octy], maps[4 * octz + 2 * octy + 1]], axis=1
                )
                for octy in range(2)
            ],
            axis=0,
        )
        wide = jnp.dot(small, jnp.asarray(chan), precision=HI)
        total = 0.0
        for pick, mask in zip(picks, masks):
            part = jnp.dot(jnp.asarray(pick), wide, precision=HI)
            total = total + jnp.where(jnp.asarray(mask), part, 0.0)
        out.append(total)
    full = jnp.stack(out)
    high = lax.reduce_precision(full, 8, 7)
    low = full - high
    return jnp.concatenate([high, high, low], axis=2).astype(BF16)


def shards(n_slab, n_pencil, owner_map, window_start, child_maps, innovation, bank,
           noise_middle, noise_finest):
    slab = lax.axis_index("slab").astype(jnp.int32)
    pencil = lax.axis_index("pencil").astype(jnp.int32)
    regions, head, tail, head_width, width = regions_of(n_slab, n_pencil)
    count = innovation.shape[0]
    owners = lax.dynamic_slice(owner_map, (window_start[0],), (BANKS,))
    info = jnp.concatenate([pencil[None], (owners == slab).astype(jnp.int32)])
    smem = pl.BlockSpec(memory_space=pltpu.SMEM)
    inner = 1
    while inner * inner < n_slab:
        inner *= 2
    outer = n_slab // inner
    cut = round_up(width // 2, LANES)
    windows = pl.pallas_call(
        functools.partial(prep_kernel, n_slab, n_pencil, cut),
        grid=(n_slab,),
        in_specs=[smem, pl.BlockSpec(bank.shape, lambda s: (0, 0, 0))],
        out_specs=[
            pl.BlockSpec((1, count, size), lambda s: ((s % inner) * outer + s // inner, 0, 0))
            for size in (cut, width - cut)
        ],
        out_shape=[
            jax.ShapeDtypeStruct((n_slab, count, size), F32) for size in (cut, width - cut)
        ],
        scratch_shapes=[pltpu.VMEM((count, LANES), F32)],
        name="windows",
    )(info, bank)
    near = [[o * inner + i for i in range(inner)] for o in range(outer)]
    far = [[o * inner + i for o in range(outer)] for i in range(inner)]
    received = []
    for parts in windows:
        parts = parts.reshape(inner, outer, count, parts.shape[2])
        parts = lax.all_to_all(parts, "slab", 0, 0, axis_index_groups=near, tiled=True)
        parts = jnp.sum(parts, axis=0)
        parts = lax.all_to_all(parts, "slab", 0, 0, axis_index_groups=far, tiled=True)
        received.append(jnp.sum(parts, axis=0))
    received = jnp.concatenate(received, axis=1)

    padded = round_up(count, 8)
    wide = round_up(padded, 16)
    maps = jnp.pad(child_maps, ((0, 0), (0, wide - count), (0, padded - count)))
    flat = jnp.concatenate(
        [maps[o] for o in range(8)]
        + [jnp.pad(innovation, ((0, wide - count), (0, wide - count)))],
        axis=1,
    )
    flat_high = lax.reduce_precision(flat, 8, 7)
    place = jnp.stack([slab, pencil])
    vmem = pl.BlockSpec(memory_space=pltpu.VMEM)
    top = regions[-1]
    upper = pl.pallas_call(
        functools.partial(chain_kernel, n_slab, n_pencil),
        in_specs=[smem, vmem, vmem, vmem],
        out_specs=vmem,
        out_shape=jax.ShapeDtypeStruct((wide, top.padded), F32),
        scratch_shapes=[pltpu.VMEM((wide, width), F32)],
        name="coarse",
    )(place, received, flat_high.astype(BF16), (flat - flat_high).astype(BF16))
    upper = upper[:count].reshape(count, top.nz, top.ny, top.nx)

    tile = 16
    half = tile // 2
    eye_rows = [[(k, y)] for k in range(count) for y in range(tile)]
    middle_weights = packed_weights(np.eye(count), eye_rows, tile, child_maps, innovation)
    _, planes, rows, cols = noise_middle.shape
    per = planes // top.nz
    octz = (slab * planes) % 2
    middle = pl.pallas_call(
        functools.partial(middle_kernel, per),
        grid=(top.nz, rows // tile),
        in_specs=[
            smem,
            pl.BlockSpec((count, 1, half, top.nx), lambda z, y: (0, z, y, 0)),
            pl.BlockSpec((count, per, tile, cols), lambda z, y: (0, z, y, 0)),
            vmem,
        ],
        out_specs=pl.BlockSpec((count, per, tile, cols), lambda z, y: (0, z, y, 0)),
        out_shape=jax.ShapeDtypeStruct(noise_middle.shape, F32),
        name="middle",
    )(octz[None], upper, noise_middle, middle_weights)

    table, row_list = fine_rows(tile)
    fine_weights = packed_weights(table, row_list, tile, child_maps, innovation)
    _, fine_planes, fine_y, fine_x = noise_finest.shape
    nz, ny = planes, fine_y // tile
    out_x = 2 * fine_x

    def block(*where):
        def index(z, y):
            at = {"z": nz - 1 - z, "y": ny - 1 - y}
            return tuple(at.get(w, 0) for w in where)

        return index

    field, zface, yface, lower, south = pl.pallas_call(
        fine_kernel,
        grid=(nz, ny),
        in_specs=[
            pl.BlockSpec((count, 1, half, cols), block(0, "z", "y", 0)),
            pl.BlockSpec((count, 2, tile, fine_x), block(0, "z", "y", 0)),
            vmem,
        ],
        out_specs=[
            pl.BlockSpec((4, 2 * tile, out_x), block("z", "y", 0)),
            pl.BlockSpec((2, 2 * tile, out_x), block("z", "y", 0)),
            pl.BlockSpec((4, tile, out_x), block("z", "y", 0)),
            pl.BlockSpec((2 * tile, out_x), block("y", 0)),
            pl.BlockSpec((1, 2, 8, out_x), block("z", 0, 0, 0)),
        ],
        out_shape=[
            jax.ShapeDtypeStruct((2 * fine_planes, 2 * fine_y, out_x), F32),
            jax.ShapeDtypeStruct((fine_planes, 2 * fine_y, out_x), F32),
            jax.ShapeDtypeStruct((2 * fine_planes, fine_y, out_x), F32),
            jax.ShapeDtypeStruct((2 * fine_y, out_x), F32),
            jax.ShapeDtypeStruct((nz, 2, 8, out_x), F32),
        ],
        scratch_shapes=[
            pltpu.VMEM((ny, 2 * tile, out_x), F32),
            pltpu.VMEM((2, 8, out_x), F32),
        ],
        name="fine",
    )(middle, noise_finest, fine_weights)
    above = shifted(lower, "slab", -1)
    beside = shifted(south[:, :, :2].reshape(2 * fine_planes, out_x), "pencil", -1)
    zface = zface.at[-1].add(above)
    yface = yface.at[:, -1].add(beside)
    return field, zface, yface


def solution(mesh):
    placed = (
        P(),
        P(),
        P(),
        P(),
        P("slab", None, None),
        P(None, "slab", "pencil", None),
        P(None, "slab", "pencil", None),
    )
    return jax.shard_map(
        functools.partial(shards, mesh.shape["slab"], mesh.shape["pencil"]),
        mesh=mesh,
        in_specs=placed,
        out_specs=(P("slab", "pencil", None), P("slab", "pencil", None), P("slab", "pencil", None)),
        check_vma=False,
    )
```
